32 devices in a mesh: mom: 4 (over y, x), sec: 8 (over z, core).
Axes of the slice: x: 2, y: 2, z: 4, core: 2. Of those that a mesh axis runs over, the one named last changes fastest.
Arguments:
- left_env: bfloat16 [64, 64, 2816], P('sec', 'mom'), may hold values from -0.75 to 0.75
- right_env: bfloat16 [64, 64, 2816], P('sec', 'mom'), may hold values from -0.109375 to 0.109375
- left_mixed: bfloat16 [4, 64, 64, 2816], P('mom', 'sec'), may hold values from -0.75 to 0.75
- excitation: bfloat16 [4, 64, 64, 256], P('mom', 'sec'), may hold values from -6 to 6
- ground: bfloat16 [64, 64, 256], P('sec'), may hold values from -6 to 6
- mpo: bfloat16 [44, 4, 44, 4], replicated, may hold values from -0.4375 to 0.4375
- momentum: int32 [4], P('mom'), may hold values from 0 to 3, each once
- block_dims: int32 [64], P('sec'), may hold values from 16 to 64, as said below
Outputs:
- excited: bfloat16 [4, 2, 64, 64, 256], P('mom', None, 'sec')
The draws below stay inside these ranges and needn't reach their ends.
Inputs may be any that keep to these rules, and one draw needn't show every extreme that they name: `block_dims`: every block has at least 16 used rows; some block uses all 64 and some exactly 16.
All inputs are finite; a program needn't handle non-finite values.
Results may differ from the reference program's by a relative error of at most 0.0058.
Values may be sent and summed in bfloat16 or wider, within the bound.
No kernel may reach another device: no remote copies, remote signals or barrier semaphores. Data moves between devices by JAX's collectives and lax.ppermute only.
A program may use at most 128 MiB of HBM per device.

```python
import math
import jax
import jax.numpy as jnp
from jax import lax

W = 44
PHYS = 4
BD = 64
NSEC = 64
N_MOMENTA = 4


def draw_block_dims(key, part):
    first, second = jax.random.split(key)
    values = jax.random.randint(first, (NSEC,), BD // 4, BD + 1)
    order = jax.random.permutation(second, NSEC)
    values = values.at[order[0]].set(BD).at[order[1]].set(BD // 4)
    return values.astype(jnp.int32)


def levels(stream_key, dims, cuts, smallest, largest):
    def one(position, parts):
        draws = jax.random.uniform(jax.random.fold_in(jax.random.fold_in(stream_key, 6), position), (parts,), jnp.float32, smallest / len(cuts), largest / len(cuts))
        return jnp.repeat(jnp.exp(draws), dims[position] // parts).reshape((-1,) + (1,) * (len(dims) - position - 1))

    loudness = one(*cuts[0])
    for cut in cuts[1:]:
        loudness = loudness * one(*cut)
    return loudness


def centred(key, extent, scale, bound, cuts=(), kind=jnp.bfloat16):
    level = levels(key, extent, cuts, -0.22, 0.18) if cuts else 1.0
    values = jax.random.normal(key, extent, jnp.float32) * scale * level
    return jnp.minimum(jnp.maximum(values, -bound), bound).astype(kind)


def setup_inputs(seed: int = 0) -> dict:
    arg_keys = jax.random.split(jax.random.key(seed), 9)
    return {
        "left_env": centred(arg_keys[0], (NSEC, BD, W * BD), BD ** -0.5, 0.75, ((0, 8), (1, 4))),
        "right_env": centred(arg_keys[1], (NSEC, BD, W * BD), (W * BD) ** -0.5, 0.109375, ((0, 8), (1, 4))),
        "left_mixed": centred(arg_keys[2], (N_MOMENTA, NSEC, BD, W * BD), BD ** -0.5, 0.75, ((0, 4), (1, 8))),
        "excitation": centred(arg_keys[3], (N_MOMENTA, NSEC, BD, PHYS * BD), 1.0, 6.0, ((0, 4), (1, 8))),
        "ground": centred(arg_keys[4], (NSEC, BD, PHYS * BD), 1.0, 6.0, ((0, 8),)),
        "mpo": centred(arg_keys[5], (W, PHYS, W, PHYS), (W * PHYS) ** -0.5, 0.4375),
        "momentum": jax.random.permutation(arg_keys[6], N_MOMENTA).astype(jnp.int32),
        "block_dims": draw_block_dims(jax.random.fold_in(arg_keys[8], 71), 0),
    }


def apply_term(left, source, right, mpo):
    width = left.shape[1]
    low = width // 3
    high = width - low
    bounds = [(0, low), (low, high), (high, width)]
    hp = lax.Precision.HIGHEST
    count = source.shape[0]
    rows = left.shape[0]
    block = right.shape[0]
    wide = source.shape[-1]
    phys = wide // block
    total = None
    for shift in range(3):
        start, stop = bounds[shift]
        temp = jnp.einsum("iwa,nab->niwb", left[:, start:stop, :].astype(jnp.float32), source[:, shift].astype(jnp.float32), precision=hp).astype(jnp.bfloat16)
        temp = temp.reshape(count, rows, stop - start, phys, block)
        part_sum = jnp.einsum("niwpj,wpvq->nviqj", temp.astype(jnp.float32), mpo[start:stop].astype(jnp.float32), precision=hp)
        total = part_sum if total is None else total + part_sum
    mixed = total.astype(jnp.bfloat16)
    result = jnp.einsum("nviqj,jvk->niqk", mixed.astype(jnp.float32), right.astype(jnp.float32), precision=hp)
    return result.reshape(count, rows, wide)


def reference(left_env, right_env, left_mixed, excitation, ground, mpo, momentum, block_dims):
    padded_ground = jnp.pad(ground, ((1, 1), (0, 0), (0, 0)))
    rows_idx = jnp.arange(BD, dtype=jnp.int32)
    cols_idx = jnp.arange(PHYS * BD, dtype=jnp.int32) % BD

    def per_momentum(index):
        padded_exc = jnp.pad(excitation[index], ((1, 1), (0, 0), (0, 0)))
        phase = 2.0 * math.pi * momentum[index].astype(jnp.float32) / N_MOMENTA

        def per_sector(sector):
            right = right_env[sector].reshape(BD, W, BD)
            left = left_env[sector].reshape(BD, W, BD)
            mixl = left_mixed[index, sector].reshape(BD, W, BD)
            src_exc = lax.dynamic_slice_in_dim(padded_exc, sector, 3, 0)[None]
            src_gr = lax.dynamic_slice_in_dim(padded_ground, sector, 3, 0)[None]
            direct = apply_term(left, src_exc, right, mpo)[0]
            shifted = apply_term(mixl, src_gr, right, mpo)[0]
            used = block_dims[sector]
            mask = ((rows_idx[:, None] < used) & (cols_idx[None, :] < used)).astype(jnp.float32)
            real_part = mask * (direct + jnp.cos(phase) * shifted)
            imag_part = -mask * jnp.sin(phase) * shifted
            return jnp.stack([real_part, imag_part]).astype(jnp.bfloat16)

        out = lax.map(per_sector, jnp.arange(NSEC, dtype=jnp.int32))
        return jnp.transpose(out, (1, 0, 2, 3))

    return lax.map(per_momentum, jnp.arange(N_MOMENTA, dtype=jnp.int32))
```

```python
import functools
import math

import jax
import jax.numpy as jnp
from jax import lax
from jax.experimental import pallas as pl
from jax.experimental.pallas import tpu as pltpu
from jax.sharding import PartitionSpec as P

BF16, F32 = jnp.bfloat16, jnp.float32
VMEM_LIMIT = 50 << 20
CHUNKS = 2


def swap(x):
    return pltpu.roll(x, 64, 1)


def low_half():
    return lax.broadcasted_iota(jnp.int32, (1, 128), 1) < 64


def segments(pairs):
    low = pairs * 2 // 3 // 2
    return [(0, low), (low, pairs - low), (pairs - low, pairs)]


def spread(l_ref, g, rows, pairs):
    for c, (lo, hi) in enumerate(segments(pairs)):
        for t in range(lo, hi):
            g[pl.ds(c * 8 + t - lo, rows, stride=24), :] = l_ref[0, :, t * 128 : (t + 1) * 128].astype(F32)


def finish_mix(mx_ref, temp, o2, out_ref, pairs):
    lane = low_half()
    wide = mx_ref.shape[0]
    for u in range(16):
        y = jnp.dot(mx_ref[...], temp[u], preferred_element_type=F32)
        for t in range(2):
            o2[t, u * wide : (u + 1) * wide, :] = y[:, t * 128 : (t + 1) * 128]
    stride = wide // 4
    for e in range(2):
        for u in range(pairs // 2):
            first = 4 * u + e
            for t in range(2):
                x = o2[t, pl.ds(first, 64, stride=stride), :]
                y = o2[t, pl.ds(first + 2, 64, stride=stride), :]
                cols = slice(u * 128, (u + 1) * 128)
                out_ref[0, e, t * 128 : t * 128 + 64, cols] = jnp.where(lane, x, swap(y)).astype(BF16)
                out_ref[0, e, t * 128 + 64 : t * 128 + 128, cols] = jnp.where(lane, swap(x), y).astype(BF16)


def shifted_kernel(pairs, l_ref, s0_ref, s1_ref, s2_ref, mx_ref, out_ref, g, lq, bd, temp, o2):
    lane = low_half()

    @pl.when(pl.program_id(0) == 0)
    def _():
        g[...] = jnp.zeros_like(g)
        bd[...] = jnp.zeros_like(bd)

    spread(l_ref, g, 64, pairs)
    for pr in range(32):
        x = g[pl.ds(pr * 48, 24), :]
        y = g[pl.ds(pr * 48 + 24, 24), :]
        e = jnp.where(lane, x, swap(y))
        o = jnp.where(lane, swap(x), y)
        u, h = pr // 2, pr % 2
        for c in range(3):
            both = jnp.concatenate([e[c * 8 : c * 8 + 8], o[c * 8 : c * 8 + 8]], 0)
            lq[c, u * 16 : (u + 1) * 16, h * 128 : (h + 1) * 128] = both.astype(BF16)
    for c, s_ref in enumerate((s0_ref, s1_ref, s2_ref)):
        for t in range(2):
            x = s_ref[0, :, t * 128 : (t + 1) * 128].astype(F32)
            y = swap(x)
            z = jnp.zeros_like(x)
            for half, here, there in ((0, x, y), (1, y, x)):
                first = jnp.where(lane, here, z).astype(BF16)
                second = jnp.where(lane, z, there).astype(BF16)
                for b in range(4):
                    cols = slice((b // 2) * 128, (b // 2) * 128 + 128)
                    bd[c * 4 + 2 * t + half, b * 64 : b * 64 + 64, cols] = first if b % 2 == 0 else second
    for c in range(3):
        for p in range(4):
            y = jnp.dot(lq[c], bd[c * 4 + p], preferred_element_type=F32).astype(BF16)
            temp[:, p * 48 + c * 16 : p * 48 + c * 16 + 16, :] = y.reshape(16, 16, 256)
    finish_mix(mx_ref, temp, o2, out_ref, pairs)


def direct_kernel(pairs, rows, count, *refs):
    l_ref, sources, (mx_ref, out_ref, g, lq, ex, temp, o2) = refs[0], refs[1 : 1 + 3 * count], refs[1 + 3 * count :]
    lane = low_half()

    @pl.when(pl.program_id(0) == 0)
    def _():
        g[...] = jnp.zeros_like(g)
        ex[...] = jnp.zeros_like(ex)

    spread(l_ref, g, rows, pairs)
    for i in range(rows):
        for c in range(3):
            x = g[i * 24 + c * 8 : i * 24 + c * 8 + 8, :]
            lq[c, i * 16 : (i + 1) * 16, :] = jnp.concatenate([x, swap(x)], 0).astype(BF16)
    quads = 16 // rows
    for c in range(3):
        parts = [(r, m) for r in sources[c * count : (c + 1) * count] for m in range(r.shape[0])]
        for mg in range(quads):
            for h in range(2):
                (ra, ma), (rb, mb) = parts[4 * mg + 2 * h], parts[4 * mg + 2 * h + 1]
                for t in range(2):
                    x = ra[ma, 0, :, t * 128 : (t + 1) * 128].astype(F32)
                    y = rb[mb, 0, :, t * 128 : (t + 1) * 128].astype(F32)
                    cols = slice(h * 128, (h + 1) * 128)
                    ex[(c * 4 + 2 * t) * quads + mg, 0:64, cols] = jnp.where(lane, x, swap(y)).astype(BF16)
                    ex[(c * 4 + 2 * t + 1) * quads + mg, 0:64, cols] = jnp.where(lane, swap(x), y).astype(BF16)
        for p in range(4):
            for mg in range(quads):
                y = jnp.dot(lq[c], ex[(c * 4 + p) * quads + mg], preferred_element_type=F32).astype(BF16)
                temp[mg * rows : (mg + 1) * rows, p * 48 + c * 16 : p * 48 + c * 16 + 16, :] = y.reshape(rows, 16, 256)
    finish_mix(mx_ref, temp, o2, out_ref, pairs)


def close_kernel(pairs, count, offs_ref, a_ref, b_ref, *refs):
    pieces, (d0_ref, d1_ref, d2_ref, d3_ref, sh_ref, rs, res, fin) = refs[:count], refs[count:]
    lane = low_half()
    for k, piece in enumerate(pieces):
        size = piece.shape[1]
        for t in range(pairs):
            at = pl.multiple_of(offs_ref[k] + t * 64, size)
            rs[pl.ds(at, size), :] = piece[0, :, t * 128 : (t + 1) * 128]
    for term, ref in enumerate((a_ref, b_ref)):
        even = jnp.dot(ref[0, 0], rs[...], preferred_element_type=F32)
        odd = jnp.dot(ref[0, 1], rs[...], preferred_element_type=F32)
        res[...] = even + swap(odd)
        for t in range(2):
            x = res[pl.ds(2 * t, 64, stride=4), :]
            y = res[pl.ds(2 * t + 1, 64, stride=4), :]
            z = jnp.where(lane, x, swap(y))
            cols = slice(t * 128, (t + 1) * 128)
            if term == 0:
                for k, d_ref in enumerate((d0_ref, d1_ref, d2_ref, d3_ref)):
                    d_ref[0, :, cols] = z[k * 16 : (k + 1) * 16].astype(BF16)
            else:
                for k in range(4):
                    fin[t, pl.ds(k, 16, stride=4), :] = z[k * 16 : (k + 1) * 16]
                sh_ref[0, :, cols] = fin[t]


def combine_kernel(count, base, ints_ref, phase_ref, sh_ref, *refs):
    pieces, out_ref, rows = refs[:count], refs[-2], refs[-1]
    for k, piece in enumerate(pieces):
        size = piece.shape[1]
        rows[pl.ds(pl.multiple_of(ints_ref[k], size), size), :] = piece[0].astype(F32)
    used = ints_ref[count + base + pl.program_id(0)]
    i = lax.broadcasted_iota(jnp.int32, (64, 256), 0)
    k = lax.broadcasted_iota(jnp.int32, (64, 256), 1) % 64
    mask = ((i < used) & (k < used)).astype(F32)
    shifted = sh_ref[0]
    out_ref[0, 0, 0] = (mask * (rows[...] + phase_ref[0] * shifted)).astype(BF16)
    out_ref[0, 1, 0] = (-mask * phase_ref[1] * shifted).astype(BF16)


def params():
    return pltpu.CompilerParams(vmem_limit_bytes=VMEM_LIMIT)


def cost(flops, moved):
    return pl.CostEstimate(flops=int(flops), bytes_accessed=int(moved), transcendentals=0)


def regroup_mpo(mpo):
    width, phys = mpo.shape[:2]
    parts = []
    for lo, hi in segments(width // 2):
        part = mpo[2 * lo : 2 * hi].reshape(hi - lo, 2, phys, width, phys)
        parts.append(jnp.pad(part, ((0, 8 - (hi - lo)), (0, 0), (0, 0), (0, 0), (0, 0))))
    x = jnp.stack(parts).transpose(5, 4, 3, 0, 2, 1)
    return x.reshape(phys * width, phys * 48)


def mix_scratch(wide, pairs):
    return [pltpu.VMEM((16, 192, 256), BF16), pltpu.VMEM((2, 16 * wide, 128), F32)]


def mix_shifted(left, source, mx):
    sectors, rows, lanes = left.shape
    pairs, wide = lanes // 128, mx.shape[0]
    window = [pl.BlockSpec((1, 64, 256), lambda s, c=c: (s + c, 0, 0)) for c in range(3)]
    return pl.pallas_call(
        functools.partial(shifted_kernel, pairs),
        grid=(sectors,),
        in_specs=[pl.BlockSpec((1, rows, lanes), lambda s: (s, 0, 0))] + window + [pl.BlockSpec(mx.shape, lambda s: (0, 0))],
        out_specs=pl.BlockSpec((1, 2, 256, lanes // 2), lambda s: (s, 0, 0, 0)),
        out_shape=jax.ShapeDtypeStruct((sectors, 2, 256, lanes // 2), BF16),
        scratch_shapes=[pltpu.VMEM((64 * 24, 128), F32), pltpu.VMEM((3, 256, 256), BF16), pltpu.VMEM((12, 256, 256), BF16)]
        + mix_scratch(wide, pairs),
        compiler_params=params(),
        cost_estimate=cost(sectors * 1.2e9, sectors * 1.8e6),
        name="mix_shifted",
    )(left, source, source, source, mx)


def mix_direct(left, sources, mx):
    sectors, rows, lanes = left.shape
    pairs, wide = lanes // 128, mx.shape[0]
    window = [
        pl.BlockSpec((src.shape[0], 1, 64, 256), lambda s, c=c: (0, s + c, 0, 0)) for c in range(3) for src in sources
    ]
    return pl.pallas_call(
        functools.partial(direct_kernel, pairs, rows, len(sources)),
        grid=(sectors,),
        in_specs=[pl.BlockSpec((1, rows, lanes), lambda s: (s, 0, 0))] + window + [pl.BlockSpec(mx.shape, lambda s: (0, 0))],
        out_specs=pl.BlockSpec((1, 2, 256, lanes // 2), lambda s: (s, 0, 0, 0)),
        out_shape=jax.ShapeDtypeStruct((sectors, 2, 256, lanes // 2), BF16),
        scratch_shapes=[
            pltpu.VMEM((rows * 24, 128), F32),
            pltpu.VMEM((3, rows * 16, 128), BF16),
            pltpu.VMEM((12 * (16 // rows), 128, 256), BF16),
        ]
        + mix_scratch(wide, pairs),
        compiler_params=params(),
        cost_estimate=cost(sectors * 1.2e9, sectors * 1.8e6),
        name="mix_direct",
    )(left, *(list(sources) * 3), mx)


def close_terms(direct, shifted, pieces, offs, base):
    count, lanes = pieces[0].shape[0], pieces[0].shape[2]
    mixed = pl.BlockSpec((1, 2, 256, lanes // 2), lambda s: (s + base, 0, 0, 0))
    return pl.pallas_call(
        functools.partial(close_kernel, lanes // 128, len(pieces)),
        grid=(count,),
        in_specs=[pl.BlockSpec(memory_space=pltpu.SMEM), mixed, mixed]
        + [pl.BlockSpec((1,) + p.shape[1:], lambda s: (s, 0, 0)) for p in pieces],
        out_specs=[pl.BlockSpec((1, 16, 256), lambda s: (s, 0, 0))] * 4 + [pl.BlockSpec((1, 64, 256), lambda s: (s, 0, 0))],
        out_shape=[jax.ShapeDtypeStruct((count, 16, 256), BF16)] * 4 + [jax.ShapeDtypeStruct((count, 64, 256), F32)],
        scratch_shapes=[pltpu.VMEM((lanes // 2, 128), BF16), pltpu.VMEM((256, 128), F32), pltpu.VMEM((2, 64, 128), F32)],
        compiler_params=params(),
        cost_estimate=cost(count * 0.6e9, count * 3.3e6),
        name="close_terms",
    )(offs, direct, shifted, *pieces)


def combine(ints, phase, shifted, pieces, base, sectors, out):
    count = shifted.shape[0]
    specs = [pl.BlockSpec(memory_space=pltpu.SMEM), pl.BlockSpec(memory_space=pltpu.SMEM)]
    specs += [pl.BlockSpec((1,) + p.shape[1:], lambda s: (s, 0, 0)) for p in (shifted, *pieces)]
    args, alias = [ints, phase, shifted, *pieces], {}
    if out is not None:
        alias = {len(args): 0}
        args.append(out)
        specs.append(pl.BlockSpec(memory_space=pl.ANY))
    return pl.pallas_call(
        functools.partial(combine_kernel, len(pieces), base),
        grid=(count,),
        in_specs=specs,
        out_specs=pl.BlockSpec((1, 2, 1, 64, 256), lambda s: (0, 0, s + base, 0, 0)),
        out_shape=jax.ShapeDtypeStruct((1, 2, sectors, 64, 256), BF16),
        scratch_shapes=[pltpu.VMEM((64, 256), F32)],
        input_output_aliases=alias,
        compiler_params=params(),
        cost_estimate=cost(count * 1e5, count * 2e5),
        name="combine",
    )(*args)


def shards(left_env, right_env, left_mixed, excitation, ground, mpo, momentum, block_dims):
    sectors = excitation.shape[1]
    groups = lax.axis_size("mom")
    mine = lax.axis_index("mom")
    rows = left_env.shape[1]
    devices = lax.axis_size("sec")
    up = [(i, i + 1) for i in range(devices - 1)]
    down = [(i + 1, i) for i in range(devices - 1)]
    partner = [[(i, i ^ k) for i in range(groups)] for k in range(4)]
    step = sectors // CHUNKS

    stacked = jnp.stack([excitation[0], ground])
    before = lax.ppermute(stacked[:, sectors - 1 :], "sec", up)
    after = lax.ppermute(stacked[:, :1], "sec", down)
    padded = jnp.concatenate([before, stacked, after], axis=1)
    own = padded[:1]
    if groups == 4:
        sources = [own] + [lax.ppermute(own, "mom", partner[k]) for k in (1, 2, 3)]
    else:
        sources = [lax.all_gather(own[0], "mom")]
    rights = []
    if groups == 4:
        for c in range(CHUNKS):
            part = right_env[c * step : (c + 1) * step]
            rights.append([part] + [lax.ppermute(part, "mom", partner[k]) for k in (1, 2, 3)])
        offs = jnp.stack([mine ^ k for k in range(4)]).astype(jnp.int32) * rows
    else:
        full = lax.all_gather(right_env, "mom", axis=1, tiled=True)
        rights = [[full[c * step : (c + 1) * step]] for c in range(CHUNKS)]
        offs = jnp.zeros((1,), jnp.int32)

    mx = regroup_mpo(mpo)
    phase = 2.0 * math.pi * momentum[0].astype(F32) / groups
    waves = jnp.stack([jnp.cos(phase), jnp.sin(phase)])
    ints = jnp.concatenate([offs, block_dims])
    shifted = mix_shifted(left_mixed[0], padded[1], mx)
    direct = mix_direct(left_env, sources, mx)
    out = None
    for c in range(CHUNKS):
        *parts, held = close_terms(direct, shifted, rights[c], offs, c * step)
        if groups == 4:
            parts = [parts[0]] + [lax.ppermute(parts[k], "mom", partner[k]) for k in (1, 2, 3)]
        else:
            whole = jnp.stack(parts, 1).reshape(step, 4, groups // 4, rows, 256)
            whole = whole.transpose(0, 2, 1, 3, 4).reshape(step, groups, rows, 256)
            parts = [lax.all_to_all(whole, "mom", 1, 2, tiled=True).reshape(step, 64, 256)]
        out = combine(ints, waves, held, parts, c * step, sectors, out)
    return out


def solution(mesh):
    return jax.shard_map(
        shards,
        mesh=mesh,
        in_specs=(
            P("sec", "mom", None),
            P("sec", "mom", None),
            P("mom", "sec", None, None),
            P("mom", "sec", None, None),
            P("sec", None, None),
            P(),
            P("mom"),
            P("sec"),
        ),
        out_specs=P("mom", None, "sec", None, None),
        check_vma=False,
    )
```

```python
import functools
import math

import jax
import jax.numpy as jnp
from jax import lax
from jax.experimental import pallas as pl
from jax.experimental.pallas import tpu as pltpu
from jax.sharding import PartitionSpec as P

BF16, F32 = jnp.bfloat16, jnp.float32
VMEM_LIMIT = 24 << 20


def swap(x):
    return pltpu.roll(x, 64, 1)


def low_half():
    return lax.broadcasted_iota(jnp.int32, (1, 128), 1) < 64


def segments(pairs):
    low = pairs * 2 // 3 // 2
    return [(0, low), (low, pairs - low), (pairs - low, pairs)]


def spread(l_ref, g, rows, pairs):
    for c, (lo, hi) in enumerate(segments(pairs)):
        for t in range(lo, hi):
            g[pl.ds(c * 8 + t - lo, rows, stride=24), :] = l_ref[0, :, t * 128 : (t + 1) * 128].astype(F32)


def finish_mix(mx_ref, temp, o2, out_ref, pairs):
    lane = low_half()
    wide = mx_ref.shape[0]
    stride = wide // 4

    def contract(group):
        for u in range(4 * group, 4 * group + 4):
            y = jnp.dot(mx_ref[...], temp[u], preferred_element_type=F32)
            for t in range(2):
                o2[group][t, (u - 4 * group) * wide : (u - 4 * group + 1) * wide, :] = y[:, t * 128 : (t + 1) * 128]

    def regroup(group):
        for e in range(2):
            for u in range(pairs // 2):
                first = 4 * u + e
                for t in range(2):
                    x = o2[group][t, pl.ds(first, 16, stride=stride), :]
                    y = o2[group][t, pl.ds(first + 2, 16, stride=stride), :]
                    row = t * 128 + group * 16
                    cols = slice(u * 128, (u + 1) * 128)
                    out_ref[0, e, row : row + 16, cols] = jnp.where(lane, x, swap(y)).astype(BF16)
                    out_ref[0, e, row + 64 : row + 80, cols] = jnp.where(lane, swap(x), y).astype(BF16)

    for group in range(4):
        contract(group)
        if group:
            regroup(group - 1)
    regroup(3)


def regroup_mpo(mpo_ref, mx_ref, pairs):
    rows, width = mpo_ref.shape
    wide, cols = mx_ref.shape
    col = lax.broadcasted_iota(jnp.int32, (cols, 1), 0)
    p = (col >= 48).astype(jnp.int32) + (col >= 96).astype(jnp.int32) + (col >= 144).astype(jnp.int32)
    rest = col - 48 * p
    w = jnp.full((cols, 1), -1, jnp.int32)
    for c, (lo, hi) in enumerate(segments(pairs)):
        pair = rest % 8
        here = (rest // 16 == c) & (pair < hi - lo)
        w = jnp.where(here, 2 * (lo + pair) + (rest // 8) % 2, w)
    source = jnp.where(w < 0, -4 * 4, (w * 4 + p) * 4)
    row = lax.broadcasted_iota(jnp.int32, (1, rows), 1)
    total = jnp.zeros((wide, cols), F32)
    for q in range(4):
        pick = (row == source + q).astype(F32).astype(BF16)
        part = lax.dot_general(mpo_ref[...], pick, (((0,), (1,)), ((), ())), preferred_element_type=F32).astype(BF16)
        place = lax.broadcasted_iota(jnp.int32, (wide, width), 0) == lax.broadcasted_iota(jnp.int32, (wide, width), 1) + q * width
        total += jnp.dot(place.astype(F32).astype(BF16), part, preferred_element_type=F32)
    mx_ref[...] = total.astype(BF16)


def shifted_kernel(pairs, l_ref, s0_ref, s1_ref, s2_ref, before_ref, after_ref, mpo_ref, out_ref, mx_ref, g, lq, bd, temp, *o2):
    lane = low_half()
    step, last = pl.program_id(0), pl.num_programs(0) - 1

    @pl.when(pl.program_id(0) == 0)
    def _():
        g[...] = jnp.zeros_like(g)
        bd[...] = jnp.zeros_like(bd)
        regroup_mpo(mpo_ref, mx_ref, pairs)

    spread(l_ref, g, 64, pairs)
    for pr in range(32):
        x = g[pl.ds(pr * 48, 24), :]
        y = g[pl.ds(pr * 48 + 24, 24), :]
        e = jnp.where(lane, x, swap(y))
        o = jnp.where(lane, swap(x), y)
        u, h = pr // 2, pr % 2
        for c in range(3):
            both = jnp.concatenate([e[c * 8 : c * 8 + 8], o[c * 8 : c * 8 + 8]], 0)
            lq[c, u * 16 : (u + 1) * 16, h * 128 : (h + 1) * 128] = both.astype(BF16)
    for c, s_ref in enumerate((s0_ref, s1_ref, s2_ref)):
        for t in range(2):
            x = s_ref[0, :, t * 128 : (t + 1) * 128].astype(F32)
            if c == 0:
                x = jnp.where(step == 0, before_ref[0, 0, :, t * 128 : (t + 1) * 128].astype(F32), x)
            if c == 2:
                x = jnp.where(step == last, after_ref[0, 0, :, t * 128 : (t + 1) * 128].astype(F32), x)
            y = swap(x)
            z = jnp.zeros_like(x)
            for half, here, there in ((0, x, y), (1, y, x)):
                first = jnp.where(lane, here, z).astype(BF16)
                second = jnp.where(lane, z, there).astype(BF16)
                for b in range(4):
                    cols = slice((b // 2) * 128, (b // 2) * 128 + 128)
                    bd[c * 4 + 2 * t + half, b * 64 : b * 64 + 64, cols] = first if b % 2 == 0 else second
    for c in range(3):
        for p in range(4):
            y = jnp.dot(lq[c], bd[c * 4 + p], preferred_element_type=F32).astype(BF16)
            temp[:, p * 48 + c * 16 : p * 48 + c * 16 + 16, :] = y.reshape(16, 16, 256)
    finish_mix(mx_ref, temp, o2, out_ref, pairs)


def direct_kernel(pairs, rows, count, *refs):
    l_ref, sources, (mx_ref, out_ref, g, lq, ex, temp, *o2) = refs[0], refs[1 : 1 + 3 * count], refs[1 + 3 * count :]
    lane = low_half()

    @pl.when(pl.program_id(0) == 0)
    def _():
        g[...] = jnp.zeros_like(g)
        ex[...] = jnp.zeros_like(ex)

    spread(l_ref, g, rows, pairs)
    for i in range(rows):
        for c in range(3):
            x = g[i * 24 + c * 8 : i * 24 + c * 8 + 8, :]
            lq[c, i * 16 : (i + 1) * 16, :] = jnp.concatenate([x, swap(x)], 0).astype(BF16)
    quads = 16 // rows
    for c in range(3):
        parts = [(r, m) for r in sources[c * count : (c + 1) * count] for m in range(r.shape[0])]
        for mg in range(quads):
            for h in range(2):
                (ra, ma), (rb, mb) = parts[4 * mg + 2 * h], parts[4 * mg + 2 * h + 1]
                for t in range(2):
                    x = ra[ma, 0, :, t * 128 : (t + 1) * 128].astype(F32)
                    y = rb[mb, 0, :, t * 128 : (t + 1) * 128].astype(F32)
                    cols = slice(h * 128, (h + 1) * 128)
                    ex[(c * 4 + 2 * t) * quads + mg, 0:64, cols] = jnp.where(lane, x, swap(y)).astype(BF16)
                    ex[(c * 4 + 2 * t + 1) * quads + mg, 0:64, cols] = jnp.where(lane, swap(x), y).astype(BF16)
        for p in range(4):
            for mg in range(quads):
                y = jnp.dot(lq[c], ex[(c * 4 + p) * quads + mg], preferred_element_type=F32).astype(BF16)
                temp[mg * rows : (mg + 1) * rows, p * 48 + c * 16 : p * 48 + c * 16 + 16, :] = y.reshape(rows, 16, 256)
    finish_mix(mx_ref, temp, o2, out_ref, pairs)


def close_kernel(pairs, spans, direct, count, mixed_ref, *refs):
    pieces, outs, (rs, res, fin) = refs[:count], refs[count:-3], refs[-3:]
    lane = low_half()

    def sector(parts, s):
        for n, k, base in parts:
            size = pieces[n].shape[1]
            start = 0 if k is None else (lax.axis_index("mom") ^ k) * size
            for t in range(pairs):
                at = pl.multiple_of(start + t * 64, size)
                rs[pl.ds(at, size), :] = pieces[n][s - base, :, t * 128 : (t + 1) * 128]
        even = jnp.dot(mixed_ref[s, 0], rs[...], preferred_element_type=F32)
        odd = jnp.dot(mixed_ref[s, 1], rs[...], preferred_element_type=F32)
        res[...] = even + swap(odd)
        for t in range(2):
            x = res[pl.ds(2 * t, 64, stride=4), :]
            y = res[pl.ds(2 * t + 1, 64, stride=4), :]
            z = jnp.where(lane, x, swap(y))
            cols = slice(t * 128, (t + 1) * 128)
            if direct:
                for k, out_ref in enumerate(outs):
                    out_ref[s, :, cols] = z[k * 16 : (k + 1) * 16].astype(BF16)
            else:
                for k in range(4):
                    fin[t, pl.ds(k, 16, stride=4), :] = z[k * 16 : (k + 1) * 16]
                outs[0][s, :, cols] = fin[t]

    for lo, hi, parts in spans:
        pl.loop(lo, hi)(functools.partial(sector, parts))


def combine_kernel(dims_ref, turn_ref, shifted_ref, *refs):
    pieces, out_ref, rows = refs[:-2], refs[-2], refs[-1]
    phase = jnp.full((8, 256), turn_ref[0], F32)
    cos, sin = jnp.cos(phase)[:1], jnp.sin(phase)[:1]
    i = lax.broadcasted_iota(jnp.int32, (64, 256), 0)
    k = lax.broadcasted_iota(jnp.int32, (64, 256), 1) % 64
    for s in range(shifted_ref.shape[0]):
        shifted = shifted_ref[s]
        for n, piece in enumerate(pieces):
            size = piece.shape[1]
            start = 0 if len(pieces) == 1 else (lax.axis_index("mom") ^ n) * size
            rows[s, pl.ds(pl.multiple_of(start, size), size), :] = piece[s].astype(F32)
        mask = ((i < dims_ref[s]) & (k < dims_ref[s])).astype(F32)
        out_ref[0, 0, s] = (mask * (rows[s] + cos * shifted)).astype(BF16)
        out_ref[0, 1, s] = (-mask * sin * shifted).astype(BF16)


def params():
    return pltpu.CompilerParams(vmem_limit_bytes=VMEM_LIMIT)


def cost(flops, moved):
    return pl.CostEstimate(flops=int(flops), bytes_accessed=int(moved), transcendentals=0)


def mix_scratch(wide, pairs):
    return [pltpu.VMEM((16, 192, 256), BF16), *[pltpu.VMEM((2, 4 * wide, 128), F32)] * 4]


def mix_shifted(left, source, before, after, mpo):
    sectors, rows, lanes = left.shape
    width, phys = mpo.shape[:2]
    pairs, wide = lanes // 128, width * phys
    near = [
        pl.BlockSpec((1, 64, 256), lambda s, c=c: (jnp.clip(s + c - 1, 0, sectors - 1), 0, 0)) for c in range(3)
    ]
    edge = pl.BlockSpec((1, 1, 64, 256), lambda s: (1, 0, 0, 0))
    return pl.pallas_call(
        functools.partial(shifted_kernel, pairs),
        grid=(sectors,),
        in_specs=[pl.BlockSpec((1, rows, lanes), lambda s: (s, 0, 0))] + near + [edge, edge, pl.BlockSpec((wide * phys, width), lambda s: (0, 0))],
        out_specs=[
            pl.BlockSpec((1, 2, 256, lanes // 2), lambda s: (s, 0, 0, 0)),
            pl.BlockSpec((wide, 48 * phys), lambda s: (0, 0)),
        ],
        out_shape=[
            jax.ShapeDtypeStruct((sectors, 2, 256, lanes // 2), BF16),
            jax.ShapeDtypeStruct((wide, 48 * phys), BF16),
        ],
        scratch_shapes=[pltpu.VMEM((64 * 24, 128), F32), pltpu.VMEM((3, 256, 256), BF16), pltpu.VMEM((12, 256, 256), BF16)]
        + mix_scratch(wide, pairs),
        compiler_params=params(),
        cost_estimate=cost(sectors * 0.12e9, sectors * 0.18e6),
        name="mix_shifted",
    )(left, source, source, source, before, after, mpo.transpose(0, 1, 3, 2).reshape(wide * phys, width))


def mix_direct(left, sources, mx):
    sectors, rows, lanes = left.shape
    pairs, wide = lanes // 128, mx.shape[0]
    window = [
        pl.BlockSpec((src.shape[0], 1, 64, 256), lambda s, c=c: (0, s + c, 0, 0)) for c in range(3) for src in sources
    ]
    return pl.pallas_call(
        functools.partial(direct_kernel, pairs, rows, len(sources)),
        grid=(sectors,),
        in_specs=[pl.BlockSpec((1, rows, lanes), lambda s: (s, 0, 0))] + window + [pl.BlockSpec(mx.shape, lambda s: (0, 0))],
        out_specs=pl.BlockSpec((1, 2, 256, lanes // 2), lambda s: (s, 0, 0, 0)),
        out_shape=jax.ShapeDtypeStruct((sectors, 2, 256, lanes // 2), BF16),
        scratch_shapes=[
            pltpu.VMEM((rows * 24, 128), F32),
            pltpu.VMEM((3, rows * 16, 128), BF16),
            pltpu.VMEM((12 * (16 // rows), 128, 256), BF16),
        ]
        + mix_scratch(wide, pairs),
        compiler_params=params(),
        cost_estimate=cost(sectors * 1.2e9, sectors * 1.8e6),
        name="mix_direct",
    )(left, *(list(sources) * 3), mx)


def close(mixed, pieces, direct):
    lanes, sectors = pieces[0][0].shape[2], mixed.shape[0]
    cuts = sorted({0, sectors} | {lo for _, _, lo in pieces})
    spans = []
    for lo, hi in zip(cuts, cuts[1:]):
        parts = [(n, k, base) for n, (p, k, base) in enumerate(pieces) if base <= lo and hi <= base + p.shape[0]]
        spans.append((lo, hi, parts))
    rows, kind, count = (16, BF16, 4) if direct else (64, F32, 1)
    vmem = pl.BlockSpec(memory_space=pltpu.VMEM)
    return pl.pallas_call(
        functools.partial(close_kernel, lanes // 128, spans, direct, len(pieces)),
        in_specs=[vmem] * (1 + len(pieces)),
        out_specs=[vmem] * count,
        out_shape=[jax.ShapeDtypeStruct((sectors, rows, 256), kind)] * count,
        scratch_shapes=[pltpu.VMEM((lanes // 2, 128), BF16), pltpu.VMEM((256, 128), F32), pltpu.VMEM((2, 64, 128), F32)],
        compiler_params=params(),
        cost_estimate=cost(sectors * 0.3e9, sectors * 1.8e6),
        name="close_direct" if direct else "close_shifted",
    )(mixed, *[p for p, _, _ in pieces])


def combine(dims, turn, shifted, pieces):
    sectors = shifted.shape[0]
    vmem, smem = pl.BlockSpec(memory_space=pltpu.VMEM), pl.BlockSpec(memory_space=pltpu.SMEM)
    return pl.pallas_call(
        combine_kernel,
        in_specs=[smem, smem] + [vmem] * (1 + len(pieces)),
        out_specs=vmem,
        out_shape=jax.ShapeDtypeStruct((1, 2, sectors, 64, 256), BF16),
        scratch_shapes=[pltpu.VMEM((sectors, 64, 256), F32)],
        compiler_params=params(),
        cost_estimate=cost(sectors * 1e5, sectors * 2e5),
        name="combine",
    )(dims, turn, shifted, *pieces)


def shards(left_env, right_env, left_mixed, excitation, ground, mpo, momentum, block_dims):
    sectors = excitation.shape[1]
    groups = lax.axis_size("mom")
    rows = left_env.shape[1]
    devices = lax.axis_size("sec")
    up = [(i, i + 1) for i in range(devices - 1)]
    down = [(i + 1, i) for i in range(devices - 1)]
    partner = [[(i, i ^ k) for i in range(groups)] for k in range(4)]
    fast = groups == 4 and sectors % 2 == 0
    hop = [functools.partial(lax.ppermute, axis_name="mom", perm=p) for p in partner]
    stacked = jnp.stack([excitation[0], ground])
    before = lax.ppermute(stacked[:, sectors - 1 :], "sec", up)
    after = lax.ppermute(stacked[:, :1], "sec", down)
    own = jnp.concatenate([before[:1], excitation, after[:1]], axis=1)
    if fast:
        half = sectors // 2
        right1, right2 = hop[1](right_env), hop[2](right_env)
        sources = [own] + [hop[k](own) for k in (1, 2, 3)]
        low3, high3 = hop[2](right1[:half]), hop[1](right2[half:])
        pieces = [(right_env, 0, 0), (right1, 1, 0), (right2, 2, 0), (low3, 3, 0), (high3, 3, half)]
    else:
        sources = [lax.all_gather(own[0], "mom")]
        pieces = [(lax.all_gather(right_env, "mom", axis=1, tiled=True), None, 0)]
    turn = 2.0 * math.pi * momentum.astype(F32) / groups
    shifted, mx = mix_shifted(left_mixed[0], ground, before, after, mpo)
    direct = mix_direct(left_env, sources, mx)
    parts = close(direct, pieces, True)
    (held,) = close(shifted, pieces, False)
    if fast:
        parts = [parts[0]] + [hop[k](parts[k]) for k in (1, 2, 3)]
    else:
        whole = jnp.stack(parts, 1).reshape(sectors, 4, groups // 4, rows, 256)
        whole = whole.transpose(0, 2, 1, 3, 4).reshape(sectors, groups, rows, 256)
        parts = [lax.all_to_all(whole, "mom", 1, 2, tiled=True).reshape(sectors, 64, 256)]
    return combine(block_dims, turn, held, parts)


def solution(mesh):
    return jax.shard_map(
        shards,
        mesh=mesh,
        in_specs=(
            P("sec", "mom", None),
            P("sec", "mom", None),
            P("mom", "sec", None, None),
            P("mom", "sec", None, None),
            P("sec", None, None),
            P(),
            P("mom"),
            P("sec"),
        ),
        out_specs=P("mom", None, "sec", None, None),
        check_vma=False,
    )
```

```python
import functools
import math

import jax
import jax.numpy as jnp
from jax import lax
from jax.experimental import pallas as pl
from jax.experimental.pallas import tpu as pltpu
from jax.sharding import PartitionSpec as P

BF16, F32 = jnp.bfloat16, jnp.float32
VMEM_LIMIT = 24 << 20
UNROLL = 2
CA = 256
CB = 256


def swap(x):
    return pltpu.roll(x, 64, 1)


def low_half():
    return lax.broadcasted_iota(jnp.int32, (1, 128), 1) < 64


def segments(pairs):
    low = pairs * 2 // 3 // 2
    return [(0, low), (low, pairs - low), (pairs - low, pairs)]


def spread(l_ref, g, rows, pairs):
    for c, (lo, hi) in enumerate(segments(pairs)):
        for t in range(lo, hi):
            g[pl.ds(c * 8 + t - lo, rows, stride=24), :] = l_ref[0, :, t * 128 : (t + 1) * 128].astype(F32)


def finish_mix(mx_ref, temp, o2, out_ref, pairs):
    lane = low_half()
    wide = mx_ref.shape[0]
    stride = wide // 4

    def contract(group):
        for u in range(4 * group, 4 * group + 4):
            y = jnp.dot(mx_ref[...], temp[u], preferred_element_type=F32)
            for t in range(2):
                o2[group][t, (u - 4 * group) * wide : (u - 4 * group + 1) * wide, :] = y[:, t * 128 : (t + 1) * 128]

    def regroup(group):
        for e in range(2):
            for u in range(pairs // 2):
                first = 4 * u + e
                for t in range(2):
                    x = o2[group][t, pl.ds(first, 16, stride=stride), :].astype(BF16)
                    y = o2[group][t, pl.ds(first + 2, 16, stride=stride), :].astype(BF16)
                    row = t * 128 + group * 16
                    cols = slice(u * 128, (u + 1) * 128)
                    out_ref[0, e, row : row + 16, cols] = jnp.where(lane, x, swap(y))
                    out_ref[0, e, row + 64 : row + 80, cols] = jnp.where(lane, swap(x), y)

    for group in range(4):
        contract(group)
        if group:
            regroup(group - 1)
    regroup(3)


def regroup_mpo(mpo_ref, mx_ref, pairs):
    rows, width = mpo_ref.shape
    wide, cols = mx_ref.shape
    col = lax.broadcasted_iota(jnp.int32, (cols, 1), 0)
    p = (col >= 48).astype(jnp.int32) + (col >= 96).astype(jnp.int32) + (col >= 144).astype(jnp.int32)
    rest = col - 48 * p
    w = jnp.full((cols, 1), -1, jnp.int32)
    for c, (lo, hi) in enumerate(segments(pairs)):
        pair = rest % 8
        here = (rest // 16 == c) & (pair < hi - lo)
        w = jnp.where(here, 2 * (lo + pair) + (rest // 8) % 2, w)
    source = jnp.where(w < 0, -4 * 4, (w * 4 + p) * 4)
    row = lax.broadcasted_iota(jnp.int32, (1, rows), 1)
    total = jnp.zeros((wide, cols), F32)
    for q in range(4):
        pick = (row == source + q).astype(F32).astype(BF16)
        part = lax.dot_general(mpo_ref[...], pick, (((0,), (1,)), ((), ())), preferred_element_type=F32).astype(BF16)
        place = lax.broadcasted_iota(jnp.int32, (wide, width), 0) == lax.broadcasted_iota(jnp.int32, (wide, width), 1) + q * width
        total += jnp.dot(place.astype(F32).astype(BF16), part, preferred_element_type=F32)
    mx_ref[...] = total.astype(BF16)


def shifted_kernel(pairs, l_ref, s0_ref, s1_ref, s2_ref, before_ref, after_ref, mpo_ref, out_ref, mx_ref, g, lq, bd, temp, *o2):
    lane = low_half()
    step, last = pl.program_id(0), pl.num_programs(0) - 1

    @pl.when(pl.program_id(0) == 0)
    def _():
        g[...] = jnp.zeros_like(g)
        regroup_mpo(mpo_ref, mx_ref, pairs)

    spread(l_ref, g, 64, pairs)
    for pr in range(32):
        x = g[pl.ds(pr * 48, 24), :]
        y = g[pl.ds(pr * 48 + 24, 24), :]
        e = jnp.where(lane, x, swap(y))
        o = jnp.where(lane, swap(x), y)
        u, h = pr // 2, pr % 2
        for c in range(3):
            both = jnp.concatenate([e[c * 8 : c * 8 + 8], o[c * 8 : c * 8 + 8]], 0)
            lq[c, (16 * h + u) * 16 : (16 * h + u + 1) * 16, :] = both.astype(BF16)
    for c, s_ref in enumerate((s0_ref, s1_ref, s2_ref)):
        for t in range(2):
            x = s_ref[0, :, t * 128 : (t + 1) * 128].astype(F32)
            if c == 0:
                x = jnp.where(step == 0, before_ref[0, 0, :, t * 128 : (t + 1) * 128].astype(F32), x)
            if c == 2:
                x = jnp.where(step == last, after_ref[0, 0, :, t * 128 : (t + 1) * 128].astype(F32), x)
            y = swap(x)
            z = jnp.zeros_like(x)
            for half, here, there in ((0, x, y), (1, y, x)):
                first = jnp.where(lane, here, z).astype(BF16)
                second = jnp.where(lane, z, there).astype(BF16)
                bd[c * 4 + 2 * t + half, 0:64, :] = first
                bd[c * 4 + 2 * t + half, 64:128, :] = second
    for c in range(3):
        for p in range(4):
            for n in range(512 // CA):
                y = jnp.dot(lq[c, n * CA : (n + 1) * CA, :], bd[c * 4 + p], preferred_element_type=F32).astype(BF16)
                u, h = n * CA // 16 % 16, n * CA // 256
                rows = slice(p * 48 + c * 16, p * 48 + c * 16 + 16)
                temp[u : u + CA // 16, rows, h * 128 : (h + 1) * 128] = y.reshape(CA // 16, 16, 128)
    finish_mix(mx_ref, temp, o2, out_ref, pairs)


def direct_kernel(pairs, rows, count, *refs):
    l_ref, sources, (mx_ref, out_ref, g, lq, ex, temp, *o2) = refs[0], refs[1 : 1 + 3 * count], refs[1 + 3 * count :]
    lane = low_half()

    @pl.when(pl.program_id(0) == 0)
    def _():
        g[...] = jnp.zeros_like(g)
        ex[...] = jnp.zeros_like(ex)

    spread(l_ref, g, rows, pairs)
    for i in range(rows):
        for c in range(3):
            x = g[i * 24 + c * 8 : i * 24 + c * 8 + 8, :]
            lq[c, i * 16 : (i + 1) * 16, :] = jnp.concatenate([x, swap(x)], 0).astype(BF16)
    quads = 16 // rows
    for c in range(3):
        parts = [(r, m) for r in sources[c * count : (c + 1) * count] for m in range(r.shape[0])]
        for mg in range(quads):
            for h in range(2):
                (ra, ma), (rb, mb) = parts[4 * mg + 2 * h], parts[4 * mg + 2 * h + 1]
                for t in range(2):
                    x = ra[ma, 0, :, t * 128 : (t + 1) * 128].astype(F32)
                    y = rb[mb, 0, :, t * 128 : (t + 1) * 128].astype(F32)
                    cols = slice(h * 128, (h + 1) * 128)
                    ex[(c * 4 + 2 * t) * quads + mg, 0:64, cols] = jnp.where(lane, x, swap(y)).astype(BF16)
                    ex[(c * 4 + 2 * t + 1) * quads + mg, 0:64, cols] = jnp.where(lane, swap(x), y).astype(BF16)
        for p in range(4):
            for mg in range(quads):
                size = min(CB, rows * 16)
                for n in range(rows * 16 // size):
                    some = lq[c, n * size : (n + 1) * size, :]
                    y = jnp.dot(some, ex[(c * 4 + p) * quads + mg], preferred_element_type=F32).astype(BF16)
                    u = mg * rows + n * size // 16
                    temp[u : u + size // 16, p * 48 + c * 16 : p * 48 + c * 16 + 16, :] = y.reshape(size // 16, 16, 256)
    finish_mix(mx_ref, temp, o2, out_ref, pairs)


def close_kernel(pairs, spans, direct, count, unroll, mixed_ref, *refs):
    pieces, outs = refs[:count], refs[count : -3 * unroll]
    scratch = refs[-3 * unroll :]
    lane = low_half()

    def sectors(parts, lo, step):
        first = lo + step * unroll
        for i in range(unroll):
            for n, k, base in parts:
                size = pieces[n].shape[1]
                start = 0 if k is None else (lax.axis_index("mom") ^ k) * size
                for t in range(pairs):
                    at = pl.multiple_of(start + t * 64, size)
                    scratch[3 * i][pl.ds(at, size), :] = pieces[n][first + i - base, :, t * 128 : (t + 1) * 128]
        for i in range(unroll):
            rs, res = scratch[3 * i : 3 * i + 2]
            even = jnp.dot(mixed_ref[first + i, 0], rs[...], preferred_element_type=F32)
            odd = jnp.dot(mixed_ref[first + i, 1], rs[...], preferred_element_type=F32)
            res[...] = even + swap(odd)
        for i in range(unroll):
            res, fin = scratch[3 * i + 1 : 3 * i + 3]
            for t in range(2):
                x = res[pl.ds(2 * t, 64, stride=4), :]
                y = res[pl.ds(2 * t + 1, 64, stride=4), :]
                z = jnp.where(lane, x, swap(y))
                cols = slice(t * 128, (t + 1) * 128)
                if direct:
                    for k, out_ref in enumerate(outs):
                        out_ref[first + i, :, cols] = z[k * 16 : (k + 1) * 16].astype(BF16)
                else:
                    for k in range(4):
                        fin[t, pl.ds(k, 16, stride=4), :] = z[k * 16 : (k + 1) * 16]
                    outs[0][first + i, :, cols] = fin[t]

    for lo, hi, parts in spans:
        pl.loop(0, (hi - lo) // unroll)(functools.partial(sectors, parts, lo))


def combine_kernel(dims_ref, turn_ref, shifted_ref, *refs):
    pieces, out_ref, rows = refs[:-2], refs[-2], refs[-1]
    phase = jnp.full((8, 256), turn_ref[0], F32)
    cos, sin = jnp.cos(phase)[:1], jnp.sin(phase)[:1]
    i = lax.broadcasted_iota(jnp.int32, (64, 256), 0)
    k = lax.broadcasted_iota(jnp.int32, (64, 256), 1) % 64
    for s in range(shifted_ref.shape[0]):
        shifted = shifted_ref[s]
        for n, piece in enumerate(pieces):
            size = piece.shape[1]
            start = 0 if len(pieces) == 1 else (lax.axis_index("mom") ^ n) * size
            rows[s, pl.ds(pl.multiple_of(start, size), size), :] = piece[s].astype(F32)
        mask = ((i < dims_ref[s]) & (k < dims_ref[s])).astype(F32)
        out_ref[0, 0, s] = (mask * (rows[s] + cos * shifted)).astype(BF16)
        out_ref[0, 1, s] = (-mask * sin * shifted).astype(BF16)


def params():
    return pltpu.CompilerParams(vmem_limit_bytes=VMEM_LIMIT)


def cost(flops, moved):
    return pl.CostEstimate(flops=int(flops), bytes_accessed=int(moved), transcendentals=0)


def mix_scratch(wide, pairs):
    return [pltpu.VMEM((16, 192, 256), BF16), *[pltpu.VMEM((2, 4 * wide, 128), F32)] * 4]


def mix_shifted(left, source, before, after, mpo):
    sectors, rows, lanes = left.shape
    width, phys = mpo.shape[:2]
    pairs, wide = lanes // 128, width * phys
    near = [
        pl.BlockSpec((1, 64, 256), lambda s, c=c: (jnp.clip(s + c - 1, 0, sectors - 1), 0, 0)) for c in range(3)
    ]
    edge = pl.BlockSpec((1, 1, 64, 256), lambda s: (1, 0, 0, 0))
    return pl.pallas_call(
        functools.partial(shifted_kernel, pairs),
        grid=(sectors,),
        in_specs=[pl.BlockSpec((1, rows, lanes), lambda s: (s, 0, 0))] + near + [edge, edge, pl.BlockSpec((wide * phys, width), lambda s: (0, 0))],
        out_specs=[
            pl.BlockSpec((1, 2, 256, lanes // 2), lambda s: (s, 0, 0, 0)),
            pl.BlockSpec((wide, 48 * phys), lambda s: (0, 0)),
        ],
        out_shape=[
            jax.ShapeDtypeStruct((sectors, 2, 256, lanes // 2), BF16),
            jax.ShapeDtypeStruct((wide, 48 * phys), BF16),
        ],
        scratch_shapes=[pltpu.VMEM((64 * 24, 128), F32), pltpu.VMEM((3, 512, 128), BF16), pltpu.VMEM((12, 128, 128), BF16)]
        + mix_scratch(wide, pairs),
        compiler_params=params(),
        cost_estimate=cost(sectors * 0.12e9, sectors * 0.18e6),
        name="mix_shifted",
    )(left, source, source, source, before, after, mpo.transpose(0, 1, 3, 2).reshape(wide * phys, width))


def mix_direct(left, sources, mx):
    sectors, rows, lanes = left.shape
    pairs, wide = lanes // 128, mx.shape[0]
    window = [
        pl.BlockSpec((src.shape[0], 1, 64, 256), lambda s, c=c: (0, s + c, 0, 0)) for c in range(3) for src in sources
    ]
    return pl.pallas_call(
        functools.partial(direct_kernel, pairs, rows, len(sources)),
        grid=(sectors,),
        in_specs=[pl.BlockSpec((1, rows, lanes), lambda s: (s, 0, 0))] + window + [pl.BlockSpec(mx.shape, lambda s: (0, 0))],
        out_specs=pl.BlockSpec((1, 2, 256, lanes // 2), lambda s: (s, 0, 0, 0)),
        out_shape=jax.ShapeDtypeStruct((sectors, 2, 256, lanes // 2), BF16),
        scratch_shapes=[
            pltpu.VMEM((rows * 24, 128), F32),
            pltpu.VMEM((3, rows * 16, 128), BF16),
            pltpu.VMEM((12 * (16 // rows), 128, 256), BF16),
        ]
        + mix_scratch(wide, pairs),
        compiler_params=params(),
        cost_estimate=cost(sectors * 1.2e9, sectors * 1.8e6),
        name="mix_direct",
    )(left, *(list(sources) * 3), mx)


def close(mixed, pieces, direct):
    lanes, sectors = pieces[0][0].shape[2], mixed.shape[0]
    cuts = sorted({0, sectors} | {lo for _, _, lo in pieces})
    spans = []
    for lo, hi in zip(cuts, cuts[1:]):
        parts = [(n, k, base) for n, (p, k, base) in enumerate(pieces) if base <= lo and hi <= base + p.shape[0]]
        spans.append((lo, hi, parts))
    rows, kind, count = (16, BF16, 4) if direct else (64, F32, 1)
    unroll = UNROLL if all((hi - lo) % UNROLL == 0 for lo, hi, _ in spans) else 1
    vmem = pl.BlockSpec(memory_space=pltpu.VMEM)
    return pl.pallas_call(
        functools.partial(close_kernel, lanes // 128, spans, direct, len(pieces), unroll),
        in_specs=[vmem] * (1 + len(pieces)),
        out_specs=[vmem] * count,
        out_shape=[jax.ShapeDtypeStruct((sectors, rows, 256), kind)] * count,
        scratch_shapes=[pltpu.VMEM((lanes // 2, 128), BF16), pltpu.VMEM((256, 128), F32), pltpu.VMEM((2, 64, 128), F32)] * unroll,
        compiler_params=params(),
        cost_estimate=cost(sectors * 0.3e9, sectors * 1.8e6),
        name="close_direct" if direct else "close_shifted",
    )(mixed, *[p for p, _, _ in pieces])


def combine(dims, turn, shifted, pieces):
    sectors = shifted.shape[0]
    vmem, smem = pl.BlockSpec(memory_space=pltpu.VMEM), pl.BlockSpec(memory_space=pltpu.SMEM)
    return pl.pallas_call(
        combine_kernel,
        in_specs=[smem, smem] + [vmem] * (1 + len(pieces)),
        out_specs=vmem,
        out_shape=jax.ShapeDtypeStruct((1, 2, sectors, 64, 256), BF16),
        scratch_shapes=[pltpu.VMEM((sectors, 64, 256), F32)],
        compiler_params=params(),
        cost_estimate=cost(sectors * 1e5, sectors * 2e5),
        name="combine",
    )(dims, turn, shifted, *pieces)


def shards(left_env, right_env, left_mixed, excitation, ground, mpo, momentum, block_dims):
    sectors = excitation.shape[1]
    groups = lax.axis_size("mom")
    rows = left_env.shape[1]
    devices = lax.axis_size("sec")
    up = [(i, i + 1) for i in range(devices - 1)]
    down = [(i + 1, i) for i in range(devices - 1)]
    partner = [[(i, i ^ k) for i in range(groups)] for k in range(4)]
    fast = groups == 4 and sectors % 2 == 0
    hop = [functools.partial(lax.ppermute, axis_name="mom", perm=p) for p in partner]
    stacked = jnp.stack([excitation[0], ground])
    before = lax.ppermute(stacked[:, sectors - 1 :], "sec", up)
    after = lax.ppermute(stacked[:, :1], "sec", down)
    own = jnp.concatenate([before[:1], excitation, after[:1]], axis=1)
    if fast:
        half = sectors // 2
        right1, right2 = hop[1](right_env), hop[2](right_env)
        sources = [own] + [hop[k](own) for k in (1, 2, 3)]
        low3, high3 = hop[2](right1[:half]), hop[1](right2[half:])
        pieces = [(right_env, 0, 0), (right1, 1, 0), (right2, 2, 0), (low3, 3, 0), (high3, 3, half)]
    else:
        sources = [lax.all_gather(own[0], "mom")]
        pieces = [(lax.all_gather(right_env, "mom", axis=1, tiled=True), None, 0)]
    turn = 2.0 * math.pi * momentum.astype(F32) / groups
    shifted, mx = mix_shifted(left_mixed[0], ground, before, after, mpo)
    direct = mix_direct(left_env, sources, mx)
    parts = close(direct, pieces, True)
    (held,) = close(shifted, pieces, False)
    if fast:
        parts = [parts[0]] + [hop[k](parts[k]) for k in (1, 2, 3)]
    else:
        whole = jnp.stack(parts, 1).reshape(sectors, 4, groups // 4, rows, 256)
        whole = whole.transpose(0, 2, 1, 3, 4).reshape(sectors, groups, rows, 256)
        parts = [lax.all_to_all(whole, "mom", 1, 2, tiled=True).reshape(sectors, 64, 256)]
    return combine(block_dims, turn, held, parts)


def solution(mesh):
    return jax.shard_map(
        shards,
        mesh=mesh,
        in_specs=(
            P("sec", "mom", None),
            P("sec", "mom", None),
            P("mom", "sec", None, None),
            P("mom", "sec", None, None),
            P("sec", None, None),
            P(),
            P("mom"),
            P("sec"),
        ),
        out_specs=P("mom", None, "sec", None, None),
        check_vma=False,
    )
```

```python
import functools
import math

import jax
import jax.numpy as jnp
from jax import lax
from jax.experimental import pallas as pl
from jax.experimental.pallas import tpu as pltpu
from jax.sharding import PartitionSpec as P

BF16, F32 = jnp.bfloat16, jnp.float32
VMEM_LIMIT = 24 << 20
UNROLL = 4
CA = 256
CB = 256


def swap(x):
    return pltpu.roll(x, 64, 1)


def low_half():
    return lax.broadcasted_iota(jnp.int32, (1, 128), 1) < 64


def segments(pairs):
    low = pairs * 2 // 3 // 2
    return [(0, low), (low, pairs - low), (pairs - low, pairs)]


def spread(l_ref, g, rows, pairs):
    for c, (lo, hi) in enumerate(segments(pairs)):
        for t in range(lo, hi):
            g[pl.ds(c * 8 + t - lo, rows, stride=24), :] = l_ref[0, :, t * 128 : (t + 1) * 128].astype(F32)


def finish_mix(mx_ref, temp, o2, out_ref, pairs):
    lane = low_half()
    wide = mx_ref.shape[0]
    stride = wide // 4

    def contract(group):
        for u in range(4 * group, 4 * group + 4):
            y = jnp.dot(mx_ref[...], temp[u], preferred_element_type=F32)
            for t in range(2):
                o2[group][t, (u - 4 * group) * wide : (u - 4 * group + 1) * wide, :] = y[:, t * 128 : (t + 1) * 128]

    def regroup(group):
        for e in range(2):
            for u in range(pairs // 2):
                first = 4 * u + e
                for t in range(2):
                    x = o2[group][t, pl.ds(first, 16, stride=stride), :].astype(BF16)
                    y = o2[group][t, pl.ds(first + 2, 16, stride=stride), :].astype(BF16)
                    row = t * 128 + group * 16
                    cols = slice(u * 128, (u + 1) * 128)
                    out_ref[0, e, row : row + 16, cols] = jnp.where(lane, x, swap(y))
                    out_ref[0, e, row + 64 : row + 80, cols] = jnp.where(lane, swap(x), y)

    for group in range(4):
        contract(group)
        if group:
            regroup(group - 1)
    regroup(3)


def regroup_mpo(mpo_ref, mx_ref, pairs):
    rows, width = mpo_ref.shape
    wide, cols = mx_ref.shape
    col = lax.broadcasted_iota(jnp.int32, (cols, 1), 0)
    p = (col >= 48).astype(jnp.int32) + (col >= 96).astype(jnp.int32) + (col >= 144).astype(jnp.int32)
    rest = col - 48 * p
    w = jnp.full((cols, 1), -1, jnp.int32)
    for c, (lo, hi) in enumerate(segments(pairs)):
        pair = rest % 8
        here = (rest // 16 == c) & (pair < hi - lo)
        w = jnp.where(here, 2 * (lo + pair) + (rest // 8) % 2, w)
    source = jnp.where(w < 0, -4 * 4, (w * 4 + p) * 4)
    row = lax.broadcasted_iota(jnp.int32, (1, rows), 1)
    total = jnp.zeros((wide, cols), F32)
    for q in range(4):
        pick = (row == source + q).astype(F32).astype(BF16)
        part = lax.dot_general(mpo_ref[...], pick, (((0,), (1,)), ((), ())), preferred_element_type=F32).astype(BF16)
        place = lax.broadcasted_iota(jnp.int32, (wide, width), 0) == lax.broadcasted_iota(jnp.int32, (wide, width), 1) + q * width
        total += jnp.dot(place.astype(F32).astype(BF16), part, preferred_element_type=F32)
    mx_ref[...] = total.astype(BF16)


def shifted_kernel(pairs, l_ref, s0_ref, s1_ref, s2_ref, before_ref, after_ref, mpo_ref, out_ref, mx_ref, g, lq, bd, temp, *o2):
    lane = low_half()
    step, last = pl.program_id(0), pl.num_programs(0) - 1

    @pl.when(pl.program_id(0) == 0)
    def _():
        g[...] = jnp.zeros_like(g)
        regroup_mpo(mpo_ref, mx_ref, pairs)

    spread(l_ref, g, 64, pairs)
    for pr in range(32):
        x = g[pl.ds(pr * 48, 24), :]
        y = g[pl.ds(pr * 48 + 24, 24), :]
        e = jnp.where(lane, x, swap(y))
        o = jnp.where(lane, swap(x), y)
        u, h = pr // 2, pr % 2
        for c in range(3):
            both = jnp.concatenate([e[c * 8 : c * 8 + 8], o[c * 8 : c * 8 + 8]], 0)
            lq[c, (16 * h + u) * 16 : (16 * h + u + 1) * 16, :] = both.astype(BF16)
    for c, s_ref in enumerate((s0_ref, s1_ref, s2_ref)):
        for t in range(2):
            x = s_ref[0, :, t * 128 : (t + 1) * 128].astype(F32)
            if c == 0:
                x = jnp.where(step == 0, before_ref[0, 0, :, t * 128 : (t + 1) * 128].astype(F32), x)
            if c == 2:
                x = jnp.where(step == last, after_ref[0, 0, :, t * 128 : (t + 1) * 128].astype(F32), x)
            y = swap(x)
            z = jnp.zeros_like(x)
            for half, here, there in ((0, x, y), (1, y, x)):
                first = jnp.where(lane, here, z).astype(BF16)
                second = jnp.where(lane, z, there).astype(BF16)
                bd[c * 4 + 2 * t + half, 0:64, :] = first
                bd[c * 4 + 2 * t + half, 64:128, :] = second
    for c in range(3):
        for p in range(4):
            for n in range(512 // CA):
                y = jnp.dot(lq[c, n * CA : (n + 1) * CA, :], bd[c * 4 + p], preferred_element_type=F32).astype(BF16)
                u, h = n * CA // 16 % 16, n * CA // 256
                rows = slice(p * 48 + c * 16, p * 48 + c * 16 + 16)
                temp[u : u + CA // 16, rows, h * 128 : (h + 1) * 128] = y.reshape(CA // 16, 16, 128)
    finish_mix(mx_ref, temp, o2, out_ref, pairs)


def direct_kernel(pairs, rows, count, *refs):
    l_ref, sources, (mx_ref, out_ref, g, lq, ex, temp, *o2) = refs[0], refs[1 : 1 + 3 * count], refs[1 + 3 * count :]
    lane = low_half()

    @pl.when(pl.program_id(0) == 0)
    def _():
        g[...] = jnp.zeros_like(g)
        ex[...] = jnp.zeros_like(ex)

    spread(l_ref, g, rows, pairs)
    for i in range(rows):
        for c in range(3):
            x = g[i * 24 + c * 8 : i * 24 + c * 8 + 8, :]
            lq[c, i * 16 : (i + 1) * 16, :] = jnp.concatenate([x, swap(x)], 0).astype(BF16)
    quads = 16 // rows
    for c in range(3):
        parts = [(r, m) for r in sources[c * count : (c + 1) * count] for m in range(r.shape[0])]
        for mg in range(quads):
            for h in range(2):
                (ra, ma), (rb, mb) = parts[4 * mg + 2 * h], parts[4 * mg + 2 * h + 1]
                for t in range(2):
                    x = ra[ma, 0, :, t * 128 : (t + 1) * 128].astype(F32)
                    y = rb[mb, 0, :, t * 128 : (t + 1) * 128].astype(F32)
                    cols = slice(h * 128, (h + 1) * 128)
                    ex[(c * 4 + 2 * t) * quads + mg, 0:64, cols] = jnp.where(lane, x, swap(y)).astype(BF16)
                    ex[(c * 4 + 2 * t + 1) * quads + mg, 0:64, cols] = jnp.where(lane, swap(x), y).astype(BF16)
        for p in range(4):
            for mg in range(quads):
                size = min(CB, rows * 16)
                for n in range(rows * 16 // size):
                    some = lq[c, n * size : (n + 1) * size, :]
                    y = jnp.dot(some, ex[(c * 4 + p) * quads + mg], preferred_element_type=F32).astype(BF16)
                    u = mg * rows + n * size // 16
                    temp[u : u + size // 16, p * 48 + c * 16 : p * 48 + c * 16 + 16, :] = y.reshape(size // 16, 16, 256)
    finish_mix(mx_ref, temp, o2, out_ref, pairs)


def close_kernel(pairs, layout, direct, unroll, mixed_ref, *refs):
    count = len(layout)
    pieces, outs = refs[:count], refs[count : -3 * unroll]
    scratch = refs[-3 * unroll :]
    lane = low_half()
    steps = mixed_ref.shape[0] // unroll

    @pl.loop(0, steps)
    def sectors(step):
        first = step * unroll
        for (k, base), piece in zip(layout, pieces):
            length, size = piece.shape[:2]
            start = 0 if k is None else (lax.axis_index("mom") ^ k) * size

            def place(piece=piece, base=base, size=size, start=start):
                for i in range(unroll):
                    for t in range(pairs):
                        at = pl.multiple_of(start + t * 64, size)
                        scratch[3 * i][pl.ds(at, size), :] = piece[first + i - base, :, t * 128 : (t + 1) * 128]

            if length == mixed_ref.shape[0]:
                place()
            else:
                pl.when((first >= base) & (first < base + length))(place)
        for i in range(unroll):
            rs, res = scratch[3 * i : 3 * i + 2]
            even = jnp.dot(mixed_ref[first + i, 0], rs[...], preferred_element_type=F32)
            odd = jnp.dot(mixed_ref[first + i, 1], rs[...], preferred_element_type=F32)
            res[...] = even + swap(odd)
        for i in range(unroll):
            res, fin = scratch[3 * i + 1 : 3 * i + 3]
            for t in range(2):
                x = res[pl.ds(2 * t, 64, stride=4), :]
                y = res[pl.ds(2 * t + 1, 64, stride=4), :]
                z = jnp.where(lane, x, swap(y))
                cols = slice(t * 128, (t + 1) * 128)
                if direct:
                    for k, out_ref in enumerate(outs):
                        out_ref[first + i, :, cols] = z[k * 16 : (k + 1) * 16].astype(BF16)
                else:
                    for k in range(4):
                        fin[t, pl.ds(k, 16, stride=4), :] = z[k * 16 : (k + 1) * 16]
                    outs[0][first + i, :, cols] = fin[t]


def combine_kernel(dims_ref, turn_ref, shifted_ref, *refs):
    pieces, out_ref, rows = refs[:-2], refs[-2], refs[-1]
    phase = jnp.full((8, 256), turn_ref[0], F32)
    cos, sin = jnp.cos(phase)[:1], jnp.sin(phase)[:1]
    i = lax.broadcasted_iota(jnp.int32, (64, 256), 0)
    k = lax.broadcasted_iota(jnp.int32, (64, 256), 1) % 64
    for s in range(shifted_ref.shape[0]):
        shifted = shifted_ref[s]
        for n, piece in enumerate(pieces):
            size = piece.shape[1]
            start = 0 if len(pieces) == 1 else (lax.axis_index("mom") ^ n) * size
            rows[s, pl.ds(pl.multiple_of(start, size), size), :] = piece[s].astype(F32)
        mask = ((i < dims_ref[s]) & (k < dims_ref[s])).astype(F32)
        out_ref[0, 0, s] = (mask * (rows[s] + cos * shifted)).astype(BF16)
        out_ref[0, 1, s] = (-mask * sin * shifted).astype(BF16)


def params():
    return pltpu.CompilerParams(vmem_limit_bytes=VMEM_LIMIT)


def cost(flops, moved):
    return pl.CostEstimate(flops=int(flops), bytes_accessed=int(moved), transcendentals=0)


def mix_scratch(wide, pairs):
    return [pltpu.VMEM((16, 192, 256), BF16), *[pltpu.VMEM((2, 4 * wide, 128), F32)] * 4]


def mix_shifted(left, source, before, after, mpo):
    sectors, rows, lanes = left.shape
    width, phys = mpo.shape[:2]
    pairs, wide = lanes // 128, width * phys
    near = [
        pl.BlockSpec((1, 64, 256), lambda s, c=c: (jnp.clip(s + c - 1, 0, sectors - 1), 0, 0)) for c in range(3)
    ]
    edge = pl.BlockSpec((1, 1, 64, 256), lambda s: (1, 0, 0, 0))
    return pl.pallas_call(
        functools.partial(shifted_kernel, pairs),
        grid=(sectors,),
        in_specs=[pl.BlockSpec((1, rows, lanes), lambda s: (s, 0, 0))] + near + [edge, edge, pl.BlockSpec((wide * phys, width), lambda s: (0, 0))],
        out_specs=[
            pl.BlockSpec((1, 2, 256, lanes // 2), lambda s: (s, 0, 0, 0)),
            pl.BlockSpec((wide, 48 * phys), lambda s: (0, 0)),
        ],
        out_shape=[
            jax.ShapeDtypeStruct((sectors, 2, 256, lanes // 2), BF16),
            jax.ShapeDtypeStruct((wide, 48 * phys), BF16),
        ],
        scratch_shapes=[pltpu.VMEM((64 * 24, 128), F32), pltpu.VMEM((3, 512, 128), BF16), pltpu.VMEM((12, 128, 128), BF16)]
        + mix_scratch(wide, pairs),
        compiler_params=params(),
        cost_estimate=cost(sectors * 0.12e9, sectors * 0.18e6),
        name="mix_shifted",
    )(left, source, source, source, before, after, mpo.transpose(0, 1, 3, 2).reshape(wide * phys, width))


def mix_direct(left, sources, mx):
    sectors, rows, lanes = left.shape
    pairs, wide = lanes // 128, mx.shape[0]
    window = [
        pl.BlockSpec((src.shape[0], 1, 64, 256), lambda s, c=c: (0, s + c, 0, 0)) for c in range(3) for src in sources
    ]
    return pl.pallas_call(
        functools.partial(direct_kernel, pairs, rows, len(sources)),
        grid=(sectors,),
        in_specs=[pl.BlockSpec((1, rows, lanes), lambda s: (s, 0, 0))] + window + [pl.BlockSpec(mx.shape, lambda s: (0, 0))],
        out_specs=pl.BlockSpec((1, 2, 256, lanes // 2), lambda s: (s, 0, 0, 0)),
        out_shape=jax.ShapeDtypeStruct((sectors, 2, 256, lanes // 2), BF16),
        scratch_shapes=[
            pltpu.VMEM((rows * 24, 128), F32),
            pltpu.VMEM((3, rows * 16, 128), BF16),
            pltpu.VMEM((12 * (16 // rows), 128, 256), BF16),
        ]
        + mix_scratch(wide, pairs),
        compiler_params=params(),
        cost_estimate=cost(sectors * 1.2e9, sectors * 1.8e6),
        name="mix_direct",
    )(left, *(list(sources) * 3), mx)


def close(mixed, pieces, direct):
    lanes, sectors = pieces[0][0].shape[2], mixed.shape[0]
    layout = [(k, base) for _, k, base in pieces]
    rows, kind, count = (16, BF16, 4) if direct else (64, F32, 1)
    unroll = UNROLL if all(p.shape[0] % UNROLL == 0 for p, _, _ in pieces) and sectors > UNROLL else 1
    vmem = pl.BlockSpec(memory_space=pltpu.VMEM)
    return pl.pallas_call(
        functools.partial(close_kernel, lanes // 128, layout, direct, unroll),
        in_specs=[vmem] * (1 + len(pieces)),
        out_specs=[vmem] * count,
        out_shape=[jax.ShapeDtypeStruct((sectors, rows, 256), kind)] * count,
        scratch_shapes=[pltpu.VMEM((lanes // 2, 128), BF16), pltpu.VMEM((256, 128), F32), pltpu.VMEM((2, 64, 128), F32)] * unroll,
        compiler_params=params(),
        cost_estimate=cost(sectors * 0.3e9, sectors * 1.8e6),
        name="close_direct" if direct else "close_shifted",
    )(mixed, *[p for p, _, _ in pieces])


def combine(dims, turn, shifted, pieces):
    sectors = shifted.shape[0]
    vmem, smem = pl.BlockSpec(memory_space=pltpu.VMEM), pl.BlockSpec(memory_space=pltpu.SMEM)
    return pl.pallas_call(
        combine_kernel,
        in_specs=[smem, smem] + [vmem] * (1 + len(pieces)),
        out_specs=vmem,
        out_shape=jax.ShapeDtypeStruct((1, 2, sectors, 64, 256), BF16),
        scratch_shapes=[pltpu.VMEM((sectors, 64, 256), F32)],
        compiler_params=params(),
        cost_estimate=cost(sectors * 1e5, sectors * 2e5),
        name="combine",
    )(dims, turn, shifted, *pieces)


def shards(left_env, right_env, left_mixed, excitation, ground, mpo, momentum, block_dims):
    sectors = excitation.shape[1]
    groups = lax.axis_size("mom")
    rows = left_env.shape[1]
    devices = lax.axis_size("sec")
    up = [(i, i + 1) for i in range(devices - 1)]
    down = [(i + 1, i) for i in range(devices - 1)]
    partner = [[(i, i ^ k) for i in range(groups)] for k in range(4)]
    fast = groups == 4 and sectors % 2 == 0
    hop = [functools.partial(lax.ppermute, axis_name="mom", perm=p) for p in partner]
    stacked = jnp.stack([excitation[0], ground])
    before = lax.ppermute(stacked[:, sectors - 1 :], "sec", up)
    after = lax.ppermute(stacked[:, :1], "sec", down)
    own = jnp.concatenate([before[:1], excitation, after[:1]], axis=1)
    if fast:
        half = sectors // 2
        right1, right2 = hop[1](right_env), hop[2](right_env)
        sources = [own] + [hop[k](own) for k in (1, 2, 3)]
        low3, high3 = hop[2](right1[:half]), hop[1](right2[half:])
        pieces = [(right_env, 0, 0), (right1, 1, 0), (right2, 2, 0), (low3, 3, 0), (high3, 3, half)]
    else:
        sources = [lax.all_gather(own[0], "mom")]
        pieces = [(lax.all_gather(right_env, "mom", axis=1, tiled=True), None, 0)]
    turn = 2.0 * math.pi * momentum.astype(F32) / groups
    shifted, mx = mix_shifted(left_mixed[0], ground, before, after, mpo)
    direct = mix_direct(left_env, sources, mx)
    parts = close(direct, pieces, True)
    (held,) = close(shifted, pieces, False)
    if fast:
        parts = [parts[0]] + [hop[k](parts[k]) for k in (1, 2, 3)]
    else:
        whole = jnp.stack(parts, 1).reshape(sectors, 4, groups // 4, rows, 256)
        whole = whole.transpose(0, 2, 1, 3, 4).reshape(sectors, groups, rows, 256)
        parts = [lax.all_to_all(whole, "mom", 1, 2, tiled=True).reshape(sectors, 64, 256)]
    return combine(block_dims, turn, held, parts)


def solution(mesh):
    return jax.shard_map(
        shards,
        mesh=mesh,
        in_specs=(
            P("sec", "mom", None),
            P("sec", "mom", None),
            P("mom", "sec", None, None),
            P("mom", "sec", None, None),
            P("sec", None, None),
            P(),
            P("mom"),
            P("sec"),
        ),
        out_specs=P("mom", None, "sec", None, None),
        check_vma=False,
    )
```
